512 devices in a mesh: expert: 64 (over y, z), dp: 8 (over x, core).
Axes of the slice: x: 4, y: 4, z: 16, core: 2. Of those that a mesh axis runs over, the one named last changes fastest.
Arguments:
- tokens: bfloat16 [2048, 2048], P('expert', 'dp'), may hold values from -6 to 6
- cotangent: bfloat16 [2048, 2048], P('expert', 'dp'), may hold values from -6 to 6
- routes: int32 [2048, 8], P('expert'), may hold values from 0 to 63, all different within a row; in each aligned block of 32 rows (0 to 31, 32 to 63, ...) at most 5 rows name the same one
- route_weights: bfloat16 [2048, 8], P('expert'), may hold values from 0.019897461 to 0.5
- gate_weight: bfloat16 [64, 1536, 2048], P('expert', 'dp'), may hold values from -6 to 6
- up_weight: bfloat16 [64, 1536, 2048], P('expert', 'dp'), may hold values from -6 to 6
- down_weight: bfloat16 [64, 1536, 2048], P('expert', 'dp'), may hold values from -6 to 6
- cluster_order: int32 [64], replicated, may hold values from 0 to 63, each once
Outputs:
- merged_gate: bfloat16 [64, 1536, 2048], P('expert', 'dp')
- merged_up: bfloat16 [64, 1536, 2048], P('expert', 'dp')
- merged_down: bfloat16 [64, 1536, 2048], P('expert', 'dp')
The draws below stay inside these ranges and needn't reach their ends.
Inputs may be any that keep to these rules, and one draw needn't show every extreme that they name: `routes`: each row names 8 different experts. Among the 32 rows of one index of expert, no expert is named more than 5 times, a bound that some block reaches. `cluster_order`: each value appears once, so every cluster has exactly 4 experts.
All inputs are finite; a program needn't handle non-finite values.
Results may differ from the reference program's by a relative error of at most 0.0085.
Values may be sent and summed in bfloat16 or wider, within the bound.
No kernel may reach another device: no remote copies, remote signals or barrier semaphores. Data moves between devices by JAX's collectives and lax.ppermute only.
A program may use at most 64 MiB of HBM per device.

```python
import math
import jax
import jax.numpy as jnp
import numpy as np
from jax import lax

D = 2048
FF = 1536
TOP = 8
MEMBERS = 4
TOK_DEV = 32
EXPERTS = 64
TOKENS = 2048
CAP = 5
CLUSTERS = 16
N_EXPERT = 64


def level_of(own_key, dims, shards, least, top_value):
    factor_of = 1.0
    for axis_at, blocks in shards:
        draws = jax.random.uniform(jax.random.fold_in(jax.random.fold_in(own_key, 6), axis_at), (blocks,), jnp.float32, least / len(shards), top_value / len(shards))
        factor_of = factor_of * jnp.repeat(jnp.exp(draws), dims[axis_at] // blocks).reshape((-1,) + (1,) * (len(dims) - 1 - axis_at))
    return factor_of


def routed_block(stream_key, own, number, rows, number_of, top, reach, lean):
    order = jax.random.permutation(stream_key, number_of)
    crowded, common = portions_of(number_of, rows * top, reach, lean, True), portions_of(number_of, rows * top, reach, lean, False)
    places = jnp.arange(number_of)

    def named(lengths, rotation):
        used = int((lengths > 0).sum())
        fixed = max(1, used // 4)
        passed = fixed + (places - fixed + rotation * (used - fixed)) % max(1, number_of - fixed)
        return jnp.zeros((number_of,), jnp.int32).at[order[jnp.where(places < fixed, places, passed)]].set(jnp.asarray(lengths, jnp.int32))

    lengths = jnp.where(number % 4 == 0, named(crowded, number // 4), named(common, number - number // 4 - 1))
    mixed = jax.random.permutation(jax.random.fold_in(own, 3), number_of)
    donor, receiver = mixed[0:number_of // 2 * 2:2], mixed[1:number_of // 2 * 2:2]
    margin = jnp.minimum(lengths[donor] - 1, reach - lengths[receiver]) // 2
    margin = jnp.where((donor == order[0]) | (receiver == order[0]) | (lengths[receiver] == 0), 0, jnp.maximum(margin, 0))
    passed = jax.random.randint(jax.random.fold_in(own, 4), (number_of // 2,), 0, 1 << 20) % (margin + 1)
    lengths = lengths.at[donor].add(-passed).at[receiver].add(passed)
    items = jnp.searchsorted(jnp.cumsum(lengths), jnp.arange(rows * top), side="right").astype(jnp.int32)
    listing = items.reshape(top, rows).T
    listing = listing[jax.random.permutation(jax.random.fold_in(own, 1), rows)]
    rotation = jax.random.randint(jax.random.fold_in(own, 2), (rows, 1), 0, top)
    return jnp.take_along_axis(listing, (jnp.arange(top)[None, :] + rotation) % top, axis=1)


def portions_of(amount, total, reach, lean, full):
    loads = [(1 << 20) // math.isqrt(grade ** lean) + 1 for grade in range(1, amount + 1)]
    largest = reach if full else min(reach, max(-(-total // amount), total * loads[0] // sum(loads)))
    least = 1 if total - largest >= amount - 1 else 0
    holding, spare = [largest] + [least] * (amount - 1), total - largest - least * (amount - 1)
    while spare > 0:
        free = [i for i in range(1, amount) if holding[i] < largest] or [i for i in range(1, amount) if holding[i] < reach]
        mass, left = sum([loads[i] for i in free]), spare
        for i in free:
            more = min(reach - holding[i], max(1, left * loads[i] // mass), spare)
            holding[i] = holding[i] + more
            spare = spare - more
    return np.array(holding)


def centred(key, extent, deviation, reach, shards=(), kind=jnp.bfloat16):
    factor_of = level_of(key, extent, shards, -0.22, 0.18) if shards else 1.0
    entries = jax.random.normal(key, extent, jnp.float32) * deviation * factor_of
    return jnp.minimum(jnp.maximum(entries, -reach), reach).astype(kind)


def setup_inputs(seed: int = 0) -> dict:
    key_of = jax.random.split(jax.random.key(seed), 9)
    tokens = centred(key_of[0], (TOKENS, D), 1.0, 6.0, ((0, 64), (1, 8)))
    cotangent = centred(key_of[1], (TOKENS, D), 1.0, 6.0, ((0, 64), (1, 8)))
    routes_keys = jax.random.split(jax.random.fold_in(key_of[2], 1), TOKENS // TOK_DEV)
    routes_turns = jax.random.permutation(jax.random.fold_in(key_of[2], 3), TOKENS // TOK_DEV)
    routes = jax.vmap(lambda own, number: routed_block(jax.random.fold_in(key_of[2], 2), own, number, TOK_DEV, EXPERTS, TOP, CAP, 1))(routes_keys, routes_turns).reshape((TOKENS, TOP))
    route_weights = jnp.clip(jnp.exp(math.log(0.5) - 3.224016 * jax.random.uniform(key_of[3], (TOKENS, TOP), jnp.float32) ** level_of(key_of[3], (TOKENS, TOP), ((0, 64),), -0.2, 0.2)), 0.019897461, 0.5).astype(jnp.bfloat16)
    gate_weight = centred(key_of[4], (EXPERTS, FF, D), 1.0, 6.0, ((0, 64), (1, 8)))
    up_weight = centred(key_of[5], (EXPERTS, FF, D), 1.0, 6.0, ((0, 64), (1, 8)))
    down_weight = centred(key_of[6], (EXPERTS, FF, D), 1.0, 6.0, ((0, 64), (1, 8)))
    cluster_order = jax.random.permutation(key_of[7], EXPERTS).astype(jnp.int32)
    return dict(tokens=tokens, cotangent=cotangent, routes=routes, route_weights=route_weights, gate_weight=gate_weight, up_weight=up_weight, down_weight=down_weight, cluster_order=cluster_order)


fisher_floor = 1e-6


def silu_parts(values_in):
    sigmoid_val = jax.nn.sigmoid(values_in)
    return values_in * sigmoid_val, sigmoid_val * (1.0 + values_in * (1.0 - sigmoid_val))


def contract_rows(left_side, right_side):
    return lax.dot_general(left_side, right_side, (((0,), (0,)), ((), ())), preferred_element_type=jnp.float32)


def project(rows_in, weight_in):
    return lax.dot_general(rows_in, weight_in, (((1,), (1,)), ((), ())), preferred_element_type=jnp.float32)


def expert_fisher(expert_id, tok_pad, cot_pad, flat_routes, weight_pad, gate_local, up_local, down_local):
    chosen = jnp.nonzero(flat_routes == expert_id, size=N_EXPERT * CAP, fill_value=TOKENS * TOP)[0].astype(jnp.int32)
    token_rows = chosen // TOP
    tok_rows = tok_pad[token_rows]
    cot_rows = cot_pad[token_rows]
    gate_scalars = weight_pad[chosen]
    gate_pre = project(tok_rows, gate_local) * (D ** -0.5)
    up_pre = project(tok_rows, up_local) * (D ** -0.5)
    silu_value, silu_slope = silu_parts(gate_pre)
    activation = silu_value * up_pre
    out_grad = (gate_scalars.astype(jnp.float32)[:, None] * cot_rows.astype(jnp.float32)).astype(jnp.bfloat16)
    act_grad = project(out_grad, down_local) * (FF ** -0.5)
    up_grad = act_grad * silu_value
    gate_grad = act_grad * up_pre * silu_slope
    tok_float = tok_rows.astype(jnp.float32)
    grad_float = out_grad.astype(jnp.float32)
    tok_sq = (tok_float * tok_float).astype(jnp.bfloat16)
    grad_sq = (grad_float * grad_float).astype(jnp.bfloat16)
    act_sq = (activation * activation).astype(jnp.bfloat16)
    gate_sq = (gate_grad * gate_grad).astype(jnp.bfloat16)
    up_sq = (up_grad * up_grad).astype(jnp.bfloat16)
    fisher_gate = contract_rows(gate_sq, tok_sq).astype(jnp.bfloat16)
    fisher_up = contract_rows(up_sq, tok_sq).astype(jnp.bfloat16)
    fisher_down = contract_rows(act_sq, grad_sq).astype(jnp.bfloat16)
    return fisher_gate, fisher_up, fisher_down


def reference(tokens, cotangent, routes, route_weights, gate_weight, up_weight, down_weight, cluster_order):
    tok_pad = jnp.concatenate([tokens, jnp.zeros((1, D), jnp.bfloat16)], axis=0)
    cot_pad = jnp.concatenate([cotangent, jnp.zeros((1, D), jnp.bfloat16)], axis=0)
    flat_routes = routes.reshape(-1)
    weight_pad = jnp.concatenate([route_weights.reshape(-1), jnp.zeros((1,), jnp.bfloat16)])
    member_list = jnp.argsort(cluster_order).astype(jnp.int32)

    def per_cluster(cluster_id):
        members = lax.dynamic_slice(member_list, (cluster_id * MEMBERS,), (MEMBERS,))
        numerator = [jnp.zeros((FF, D), jnp.float32) for matrix_id in range(3)]
        denominator = [jnp.zeros((FF, D), jnp.float32) for matrix_id in range(3)]
        for position in range(MEMBERS):
            expert_id = members[position]
            weight_set = (gate_weight[expert_id], up_weight[expert_id], down_weight[expert_id])
            fishers = expert_fisher(expert_id, tok_pad, cot_pad, flat_routes, weight_pad,
                                    weight_set[0], weight_set[1], weight_set[2])
            for matrix_id in range(3):
                fisher_value = fishers[matrix_id].astype(jnp.float32)
                numerator[matrix_id] = numerator[matrix_id] + fisher_value * weight_set[matrix_id].astype(jnp.float32)
                denominator[matrix_id] = denominator[matrix_id] + fisher_value
        return tuple((numerator[matrix_id] / (denominator[matrix_id] + fisher_floor)).astype(jnp.bfloat16)
                     for matrix_id in range(3))

    cluster_gate, cluster_up, cluster_down = lax.map(per_cluster, jnp.arange(CLUSTERS, dtype=jnp.int32))
    cluster_ids = (cluster_order // MEMBERS).astype(jnp.int32)
    return cluster_gate[cluster_ids], cluster_up[cluster_ids], cluster_down[cluster_ids]
```

```python
import jax
import jax.numpy as jnp
from jax import lax
from jax.experimental import pallas as pl
from jax.experimental.pallas import tpu as pltpu
from jax.sharding import PartitionSpec as P

D = 2048
FF = 1536
MEMBERS = 4
EXPERTS = 64
CLUSTERS = 16
ROWS = 3
KINDS = 3 * ROWS
LANES = 128
TILES = D // LANES
BLOCK = 32
WIDTH = 256
Y, Z = 4, 16
fisher_floor = 1e-06
VMEM_LIMIT = 60 * 1024 * 1024


def swap_matrix():
    row = lax.broadcasted_iota(jnp.int32, (256, 256), 0)
    col = lax.broadcasted_iota(jnp.int32, (256, 256), 1)
    hit = (row // 16 == col % 16) & (row % 16 == col // 16)
    return jnp.where(hit, 1.0, 0.0).astype(jnp.bfloat16)


def dot(left, right):
    return jnp.dot(left, right, preferred_element_type=jnp.float32)


def dot_t(left, right):
    return lax.dot_general(
        left, right, (((1,), (1,)), ((), ())), preferred_element_type=jnp.float32
    )


def pack_kernel(gate, up, down, out):
    swap = swap_matrix()
    for m, ref in enumerate((gate, up, down)):
        for j in range(ROWS):
            for kb in range(4):
                rows = slice(64 * j + 16 * kb, 64 * j + 16 * kb + 16)
                stacked = jnp.concatenate(
                    [ref[rows, l * LANES : (l + 1) * LANES] for l in range(TILES)], axis=0
                )
                turned = dot(swap, stacked).astype(jnp.bfloat16)
                q = m * ROWS + j
                out[16 * kb : 16 * kb + 16, 16 * q : 16 * q + 16, :] = turned.reshape(
                    16, 16, LANES
                )


def unpack_kernel(packed, gate, up, down):
    swap = swap_matrix()
    for m, ref in enumerate((gate, up, down)):
        for j in range(ROWS):
            for kb in range(4):
                q = m * ROWS + j
                stacked = packed[16 * kb : 16 * kb + 16, 16 * q : 16 * q + 16, :].reshape(
                    256, LANES
                )
                turned = dot(swap, stacked).astype(jnp.bfloat16)
                rows = slice(64 * j + 16 * kb, 64 * j + 16 * kb + 16)
                for l in range(TILES):
                    ref[rows, l * LANES : (l + 1) * LANES] = turned[16 * l : 16 * l + 16]


def merge_kernel(*refs):
    (packed, route_map, members, spread) = refs[:4]
    pieces = refs[4:14]
    out, tok, cot, weights, fisher_rows, merged, sems = refs[14:]
    place = lax.axis_index("dp")
    x, core = place // 2, place % 2
    copies = []
    for side in range(2):
        c = core if side == 0 else 1 - core
        for i, (shift, first) in enumerate(((0, 0), (3, 0), (1, 0), (2, 0), (2, 32))):
            piece = pieces[5 * side + i]
            lane = pl.multiple_of((((x + shift) % 4) * 2 + c) * WIDTH, WIDTH)
            blocks = piece.shape[0]
            for h, target in enumerate((tok, cot)):
                copy = pltpu.make_async_copy(
                    piece.at[:, h * BLOCK : (h + 1) * BLOCK, :],
                    target.at[first : first + blocks, :, pl.ds(lane, WIDTH)],
                    sems.at[2 * (5 * side + i) + h],
                )
                copy.start()
                copies.append(copy)
    swap = swap_matrix()
    for q in range(KINDS):
        for eb in range(4):
            stacked = packed[16 * eb : 16 * eb + 16, 16 * q : 16 * q + 16, :].reshape(256, LANES)
            turned = dot(swap, stacked).astype(jnp.bfloat16)
            rows = slice(64 * q + 16 * eb, 64 * q + 16 * eb + 16)
            for l in range(TILES):
                weights[rows, l * LANES : (l + 1) * LANES] = turned[16 * l : 16 * l + 16]
    for copy in copies:
        copy.wait()
    third = ROWS * EXPERTS

    def project(t, carry):
        at = pl.multiple_of(t * 8, 8)
        tok_rows = tok[pl.ds(at, 8)].reshape(256, D)
        cot_rows = cot[pl.ds(at, 8)].reshape(256, D)
        lane = pl.multiple_of(t * 256, 256)
        share = route_map[:, pl.ds(lane, 256)]
        share = jnp.concatenate([share] * ROWS, axis=0)
        pre = dot_t(weights[0 : 2 * third, :], tok_rows) * (D**-0.5)
        act_grad = dot_t(weights[2 * third :, :], cot_rows) * (FF**-0.5) * share
        gate_pre, up_pre = pre[:third], pre[third:]
        sigmoid = jax.nn.sigmoid(gate_pre)
        silu = gate_pre * sigmoid
        slope = sigmoid * (1.0 + gate_pre * (1.0 - sigmoid))
        gate_grad = act_grad * up_pre * slope
        up_grad = act_grad * silu
        act = silu * up_pre * share
        for m, value in enumerate((gate_grad, up_grad, act)):
            fisher_rows[m * third : (m + 1) * third, pl.ds(lane, 256)] = (value * value).astype(
                jnp.bfloat16
            )
        return carry

    lax.fori_loop(0, 8, project, 0)

    def merge(f, carry):
        lane = pl.multiple_of(f * WIDTH, WIDTH)
        tok_cols = tok[:, :, pl.ds(lane, WIDTH)].reshape(2048, WIDTH)
        cot_cols = cot[:, :, pl.ds(lane, WIDTH)].reshape(2048, WIDTH)
        fisher_in = dot(fisher_rows[0 : 2 * third, :], tok_cols * tok_cols)
        fisher_down = dot(fisher_rows[2 * third :, :], cot_cols * cot_cols)
        fisher = jnp.concatenate(
            [fisher_in.astype(jnp.bfloat16), fisher_down.astype(jnp.bfloat16)], axis=0
        )
        product = fisher.astype(jnp.float32) * weights[:, pl.ds(lane, WIDTH)].astype(jnp.float32)
        high = product.astype(jnp.bfloat16)
        low = (product - high.astype(jnp.float32)).astype(jnp.bfloat16)
        table = members[...]
        numerator = dot(table, high) + dot(table, low)
        denominator = dot(table, fisher)
        merged[:, pl.ds(lane, WIDTH)] = (numerator / (denominator + fisher_floor)).astype(
            jnp.bfloat16
        )
        return carry

    lax.fori_loop(0, 8, merge, 0)
    for q in range(KINDS):
        stacked = jnp.concatenate(
            [merged[16 * q : 16 * q + 16, l * LANES : (l + 1) * LANES] for l in range(TILES)], axis=0
        )
        for eb in range(4):
            turned = dot(spread[256 * eb : 256 * eb + 256, :], stacked).astype(jnp.bfloat16)
            out[16 * eb : 16 * eb + 16, 16 * q : 16 * q + 16, :] = turned.reshape(16, 16, LANES)


def params():
    return pltpu.CompilerParams(vmem_limit_bytes=VMEM_LIMIT)


PACKED = jax.ShapeDtypeStruct((EXPERTS, KINDS * TILES, LANES), jnp.bfloat16)


def expert_pairs(move):
    return [(y * Z + z, move(y, z)[0] * Z + move(y, z)[1]) for y in range(Y) for z in range(Z)]


def dp_pairs(move):
    return [(2 * x + c, move(x, c)[0] * 2 + move(x, c)[1]) for x in range(4) for c in range(2)]


def gather_ring(value, axis, up, down):
    half = value.shape[0] // 2
    before = lax.ppermute(value, axis, up)
    after = lax.ppermute(value, axis, down)
    far_first = lax.ppermute(before[:half], axis, up)
    far_last = lax.ppermute(after[half:], axis, down)
    return value, before, after, far_first, far_last


def body(
    tokens, cotangent, routes, route_weights, gate_weight, up_weight, down_weight, cluster_order
):
    hidden = gate_weight.shape[1]
    whole = pl.BlockSpec(memory_space=pltpu.VMEM)
    packed = pl.pallas_call(
        pack_kernel, out_shape=PACKED, in_specs=[whole] * 3, out_specs=whole,
        compiler_params=params(), name="pack",
    )(gate_weight[0], up_weight[0], down_weight[0])
    received = lax.all_to_all(packed, "expert", split_axis=0, concat_axis=0, tiled=True)

    chosen = routes[:, :, None] == jnp.arange(EXPERTS, dtype=jnp.int32)[None, None, :]
    share = jnp.sum(jnp.where(chosen, route_weights.astype(jnp.float32)[:, :, None], 0.0), axis=1)
    share = share.astype(jnp.bfloat16)
    share = jnp.concatenate([share[8 * i : 8 * i + 8] for i in range(4)], axis=1)
    block = jnp.concatenate([tokens, cotangent, share], axis=0)[None]
    for bit in (8, 4, 2, 1):
        other = lax.ppermute(block, "expert", expert_pairs(lambda y, z: (y, z ^ bit)))
        block = jnp.concatenate([block, other], axis=0)
    ring = gather_ring(
        block, "expert",
        expert_pairs(lambda y, z: ((y + 1) % Y, z)), expert_pairs(lambda y, z: ((y - 1) % Y, z)),
    )
    block = jnp.concatenate(ring, axis=0)
    share = block[:, 2 * BLOCK :, :].reshape(EXPERTS, 8, 4, EXPERTS).transpose(3, 0, 2, 1)
    share = share.reshape(EXPERTS, EXPERTS * BLOCK).astype(jnp.float32)
    near = gather_ring(
        block[:, : 2 * BLOCK, :], "dp",
        dp_pairs(lambda x, c: ((x + 1) % 4, c)), dp_pairs(lambda x, c: ((x - 1) % 4, c)),
    )
    across = dp_pairs(lambda x, c: (x, 1 - c))
    pieces = near + tuple(lax.ppermute(piece, "dp", across) for piece in near)

    cluster = cluster_order // MEMBERS
    belongs = cluster[None, :] == jnp.arange(CLUSTERS, dtype=jnp.int32)[:, None]
    members = jnp.einsum("qp,ce->qcpe", jnp.eye(KINDS), belongs.astype(jnp.float32))
    members = members.reshape(KINDS * CLUSTERS, KINDS * EXPERTS).astype(jnp.bfloat16)
    spread = jnp.einsum("lm,ce->elmc", jnp.eye(TILES), belongs.astype(jnp.float32))
    spread = spread.reshape(EXPERTS * TILES, TILES * CLUSTERS).astype(jnp.bfloat16)

    anywhere = pl.BlockSpec(memory_space=pl.ANY)
    answer = pl.pallas_call(
        merge_kernel, out_shape=PACKED, in_specs=[whole] * 4 + [anywhere] * 10, out_specs=whole,
        scratch_shapes=[
            pltpu.VMEM((EXPERTS, BLOCK, D), jnp.bfloat16),
            pltpu.VMEM((EXPERTS, BLOCK, D), jnp.bfloat16),
            pltpu.VMEM((KINDS * EXPERTS, D), jnp.bfloat16),
            pltpu.VMEM((KINDS * EXPERTS, EXPERTS * BLOCK), jnp.bfloat16),
            pltpu.VMEM((KINDS * CLUSTERS, D), jnp.bfloat16),
            pltpu.SemaphoreType.DMA((20,)),
        ],
        compiler_params=params(), name="merge",
    )(received, share, members, spread, *pieces)
    returned = lax.all_to_all(answer, "expert", split_axis=0, concat_axis=0, tiled=True)
    part = jax.ShapeDtypeStruct((hidden, D), jnp.bfloat16)
    outs = pl.pallas_call(
        unpack_kernel, out_shape=(part,) * 3, in_specs=[whole], out_specs=(whole,) * 3,
        compiler_params=params(), name="unpack",
    )(returned)
    return tuple(o[None] for o in outs)


def solution(mesh):
    return jax.shard_map(
        body,
        mesh=mesh,
        in_specs=(
            P("expert", "dp"),
            P("expert", "dp"),
            P("expert", None),
            P("expert", None),
            P("expert", "dp", None),
            P("expert", "dp", None),
            P("expert", "dp", None),
            P(),
        ),
        out_specs=(P("expert", "dp", None), P("expert", "dp", None), P("expert", "dp", None)),
        check_vma=False,
    )
```

```python
import jax
import jax.numpy as jnp
from jax import lax
from jax.experimental import pallas as pl
from jax.experimental.pallas import tpu as pltpu
from jax.sharding import PartitionSpec as P

D = 2048
FF = 1536
MEMBERS = 4
EXPERTS = 64
CLUSTERS = 16
ROWS = 3
PARTS = ((0, 1, 2),)
LANES = 128
TILES = D // LANES
BLOCK = 32
WIDTH = 256
Y, Z = 4, 16
fisher_floor = 1e-06
VMEM_LIMIT = 60 * 1024 * 1024


def swap_matrix():
    row = lax.broadcasted_iota(jnp.int32, (256, 256), 0)
    col = lax.broadcasted_iota(jnp.int32, (256, 256), 1)
    hit = (row // 16 == col % 16) & (row % 16 == col // 16)
    return jnp.where(hit, 1.0, 0.0).astype(jnp.bfloat16)


def dot(left, right):
    return jnp.dot(left, right, preferred_element_type=jnp.float32)


def dot_t(left, right):
    return lax.dot_general(
        left, right, (((1,), (1,)), ((), ())), preferred_element_type=jnp.float32
    )


def picks(rows, cols, of_row):
    row = lax.broadcasted_iota(jnp.int32, (rows, cols), 0)
    col = lax.broadcasted_iota(jnp.int32, (rows, cols), 1)
    return jnp.where(of_row(row) == col, 1.0, 0.0).astype(jnp.bfloat16)


def member_table(belongs):
    shape = (belongs.shape[1] // EXPERTS * CLUSTERS, belongs.shape[1])
    filled = dot(picks(shape[0], CLUSTERS, lambda r: r % CLUSTERS), belongs)
    row = lax.broadcasted_iota(jnp.int32, shape, 0)
    col = lax.broadcasted_iota(jnp.int32, shape, 1)
    return jnp.where(row // CLUSTERS == col // EXPERTS, filled, 0.0).astype(jnp.bfloat16)


def spread_table(belongs):
    shape = (EXPERTS * TILES, TILES * CLUSTERS)
    filled = dot(picks(shape[0], EXPERTS, lambda r: r // TILES), belongs)
    row = lax.broadcasted_iota(jnp.int32, shape, 0)
    col = lax.broadcasted_iota(jnp.int32, shape, 1)
    return jnp.where(row % TILES == col // CLUSTERS, filled, 0.0).astype(jnp.bfloat16)


def parts_of():
    for part, groups in enumerate(PARTS):
        for m in range(3):
            for i, j in enumerate(groups):
                yield part, m * len(groups) + i, m, j


def pack_kernel(*refs):
    swap = swap_matrix()
    for part, q, m, j in parts_of():
        for kb in range(4):
            rows = slice(64 * j + 16 * kb, 64 * j + 16 * kb + 16)
            stacked = jnp.concatenate(
                [refs[m][rows, l * LANES : (l + 1) * LANES] for l in range(TILES)], axis=0
            )
            turned = dot(swap, stacked).astype(jnp.bfloat16)
            refs[3 + part][16 * kb : 16 * kb + 16, 16 * q : 16 * q + 16, :] = turned.reshape(
                16, 16, LANES
            )


def unpack_kernel(*refs):
    swap = swap_matrix()
    for part, q, m, j in parts_of():
        for kb in range(4):
            stacked = refs[part][16 * kb : 16 * kb + 16, 16 * q : 16 * q + 16, :]
            turned = dot(swap, stacked.reshape(256, LANES)).astype(jnp.bfloat16)
            rows = slice(64 * j + 16 * kb, 64 * j + 16 * kb + 16)
            for l in range(TILES):
                refs[len(PARTS) + m][rows, l * LANES : (l + 1) * LANES] = turned[
                    16 * l : 16 * l + 16
                ]


def merge_kernel(*refs):
    (packed, route_map, belongs_row, belongs_col) = refs[:4]
    pieces = refs[4:24]
    out, tok, cot, weights, fisher_rows, merged, sems = refs[24:]
    kinds = packed.shape[1] // TILES
    place = lax.axis_index("dp")
    x, core = place // 2, place % 2
    shifts = (0, 3, 1, 2)

    def bring(piece, target, first, shift, c, which, t):
        lane = pl.multiple_of((((x + shift) % 4) * 2 + c) * WIDTH, WIDTH)
        pltpu.make_async_copy(
            piece, target.at[first : first + piece.shape[0], :, pl.ds(lane, WIDTH)],
            sems.at[which, t],
        ).start()

    for t in range(8):
        for side in range(2):
            c = core if side == 0 else 1 - core
            tok_pieces = pieces[10 * side : 10 * side + 5]
            cot_pieces = pieces[10 * side + 5 : 10 * side + 10]
            for i in range(3):
                bring(tok_pieces[i].at[8 * t : 8 * t + 8], tok, 8 * t, shifts[i], c, 0, t)
            far = 8 * (t % 4)
            bring(tok_pieces[3 + t // 4].at[far : far + 8], tok, 8 * t, shifts[3], c, 0, t)
            for h in range(4):
                if t < 6:
                    piece, at = cot_pieces[t // 2], h
                else:
                    piece, at = cot_pieces[3 + h // 2], h % 2
                first = 16 * at + 8 * (t % 2)
                bring(piece.at[first : first + 8], cot, 8 * t, shifts[h], c, 1, t)

    def ready(t):
        for which, target in enumerate((tok, cot)):
            rows = target.at[8 * t : 8 * t + 8]
            pltpu.make_async_copy(rows, rows, sems.at[which, t]).wait()

    swap = swap_matrix()
    for q in range(kinds):
        for eb in range(4):
            stacked = packed[16 * eb : 16 * eb + 16, 16 * q : 16 * q + 16, :].reshape(256, LANES)
            turned = dot(swap, stacked).astype(jnp.bfloat16)
            rows = slice(64 * q + 16 * eb, 64 * q + 16 * eb + 16)
            for l in range(TILES):
                weights[rows, l * LANES : (l + 1) * LANES] = turned[16 * l : 16 * l + 16]
    third = kinds // 3 * EXPERTS
    table = member_table(belongs_row[...])

    def project(t):
        ready(t)
        at = 8 * t
        tok_rows = tok[pl.ds(at, 8)].reshape(256, D)
        cot_rows = cot[pl.ds(at, 8)].reshape(256, D)
        lane = 256 * t
        share = route_map[:, pl.ds(lane, 256)]
        share = jnp.concatenate([share] * (kinds // 3), axis=0)
        pre = dot_t(weights[0 : 2 * third, :], tok_rows) * (D**-0.5)
        act_grad = dot_t(weights[2 * third :, :], cot_rows) * (FF**-0.5) * share
        gate_pre, up_pre = pre[:third], pre[third:]
        sigmoid = jax.nn.sigmoid(gate_pre)
        silu = gate_pre * sigmoid
        slope = sigmoid * (1.0 + gate_pre * (1.0 - sigmoid))
        gate_grad = act_grad * up_pre * slope
        up_grad = act_grad * silu
        act = silu * up_pre * share
        for m, value in enumerate((gate_grad, up_grad, act)):
            fisher_rows[m * third : (m + 1) * third, pl.ds(lane, 256)] = (value * value).astype(
                jnp.bfloat16
            )

    for t in range(8):
        project(t)

    def merge(f):
        lane = f * WIDTH
        tok_cols = tok[:, :, pl.ds(lane, WIDTH)].reshape(2048, WIDTH)
        cot_cols = cot[:, :, pl.ds(lane, WIDTH)].reshape(2048, WIDTH)
        fisher_in = dot(fisher_rows[0 : 2 * third, :], tok_cols * tok_cols)
        fisher_down = dot(fisher_rows[2 * third :, :], cot_cols * cot_cols)
        fisher = jnp.concatenate(
            [fisher_in.astype(jnp.bfloat16), fisher_down.astype(jnp.bfloat16)], axis=0
        )
        product = fisher.astype(jnp.float32) * weights[:, pl.ds(lane, WIDTH)].astype(jnp.float32)
        high = product.astype(jnp.bfloat16)
        low = (product - high.astype(jnp.float32)).astype(jnp.bfloat16)
        numerator = dot(table, high) + dot(table, low)
        denominator = dot(table, fisher)
        merged[:, pl.ds(lane, WIDTH)] = (numerator / (denominator + fisher_floor)).astype(
            jnp.bfloat16
        )

    for f in range(8):
        merge(f)
    spread = spread_table(belongs_col[...])
    for q in range(kinds):
        stacked = jnp.concatenate(
            [merged[16 * q : 16 * q + 16, l * LANES : (l + 1) * LANES] for l in range(TILES)], axis=0
        )
        for eb in range(4):
            turned = dot(spread[256 * eb : 256 * eb + 256], stacked).astype(jnp.bfloat16)
            out[16 * eb : 16 * eb + 16, 16 * q : 16 * q + 16, :] = turned.reshape(16, 16, LANES)


def params():
    return pltpu.CompilerParams(vmem_limit_bytes=VMEM_LIMIT)


def packed_shape(kinds):
    return jax.ShapeDtypeStruct((EXPERTS, kinds * TILES, LANES), jnp.bfloat16)


def expert_pairs(move):
    return [(y * Z + z, move(y, z)[0] * Z + move(y, z)[1]) for y in range(Y) for z in range(Z)]


def dp_pairs(move):
    return [(2 * x + c, move(x, c)[0] * 2 + move(x, c)[1]) for x in range(4) for c in range(2)]


def gather_ring(value, axis, up, down):
    half = value.shape[0] // 2
    before = lax.ppermute(value, axis, up)
    after = lax.ppermute(value, axis, down)
    far_first = lax.ppermute(before[:half], axis, up)
    far_last = lax.ppermute(after[half:], axis, down)
    return value, before, after, far_first, far_last


def body(
    tokens, cotangent, routes, route_weights, gate_weight, up_weight, down_weight, cluster_order
):
    hidden = gate_weight.shape[1]
    whole = pl.BlockSpec(memory_space=pltpu.VMEM)
    shapes = tuple(packed_shape(3 * len(groups)) for groups in PARTS)
    packed = pl.pallas_call(
        pack_kernel, out_shape=shapes, in_specs=[whole] * 3, out_specs=(whole,) * len(PARTS),
        compiler_params=params(), name="pack",
    )(gate_weight[0], up_weight[0], down_weight[0])
    cluster = cluster_order // MEMBERS
    clusters = jnp.arange(CLUSTERS, dtype=jnp.int32)
    belongs_col = (cluster[:, None] == jnp.tile(clusters, TILES)[None, :]).astype(jnp.bfloat16)
    belongs_row = (clusters[:, None] == jnp.tile(cluster, 3 * ROWS)[None, :]).astype(jnp.bfloat16)

    chosen = routes[:, :, None] == jnp.arange(EXPERTS, dtype=jnp.int32)[None, None, :]
    share = jnp.sum(jnp.where(chosen, route_weights.astype(jnp.float32)[:, :, None], 0.0), axis=1)
    share = share.astype(jnp.bfloat16)
    share = jnp.concatenate([share[8 * i : 8 * i + 8] for i in range(4)], axis=1)
    block = jnp.concatenate([tokens, share, cotangent], axis=0)[None]

    def along_z(value, shift):
        return lax.ppermute(value, "expert", expert_pairs(lambda y, z: (y, (z + shift) % Z)))

    for moves in ((4, 8, 12), (1, -1, 2)):
        block = jnp.concatenate([block] + [along_z(block, shift) for shift in moves], axis=0)
    packed, block, belongs_row, belongs_col = lax.optimization_barrier(
        (packed, block, belongs_row, belongs_col)
    )

    def along_y(value):
        return gather_ring(
            value, "expert",
            expert_pairs(lambda y, z: ((y + 1) % Y, z)), expert_pairs(lambda y, z: ((y - 1) % Y, z)),
        )

    def along_x(value):
        return gather_ring(
            value, "dp",
            dp_pairs(lambda x, c: ((x + 1) % 4, c)), dp_pairs(lambda x, c: ((x - 1) % 4, c)),
        )

    received = []
    for part in packed:
        received.append(lax.all_to_all(part, "expert", split_axis=0, concat_axis=0, tiled=True))
    tok_block = jnp.concatenate(along_y(block[:, : BLOCK + 8]), axis=0)
    cot_block = jnp.concatenate(along_x(block[:, BLOCK + 8 :]), axis=0)
    share = tok_block[:, BLOCK:].reshape(EXPERTS, 8, 4, EXPERTS).transpose(3, 0, 2, 1)
    share = share.reshape(EXPERTS, EXPERTS * BLOCK).astype(jnp.float32)
    near = along_x(tok_block[:, :BLOCK]) + along_y(cot_block)
    across = dp_pairs(lambda x, c: (x, 1 - c))
    pieces = near + tuple(lax.ppermute(piece, "dp", across) for piece in near)

    anywhere = pl.BlockSpec(memory_space=pl.ANY)
    returned = []
    for n, part in enumerate(received):
        kinds = 3 * len(PARTS[n])
        answer = pl.pallas_call(
            merge_kernel, out_shape=shapes[n],
            in_specs=[whole] * 4 + [anywhere] * 20, out_specs=whole,
            scratch_shapes=[
                pltpu.VMEM((EXPERTS, BLOCK, D), jnp.bfloat16),
                pltpu.VMEM((EXPERTS, BLOCK, D), jnp.bfloat16),
                pltpu.VMEM((kinds * EXPERTS, D), jnp.bfloat16),
                pltpu.VMEM((kinds * EXPERTS, EXPERTS * BLOCK), jnp.bfloat16),
                pltpu.VMEM((kinds * CLUSTERS, D), jnp.bfloat16),
                pltpu.SemaphoreType.DMA((2, 8)),
            ],
            compiler_params=params(),
        )(part, share, belongs_row[:, : kinds * EXPERTS], belongs_col, *pieces)
        returned.append(lax.all_to_all(answer, "expert", split_axis=0, concat_axis=0, tiled=True))
    rows = jax.ShapeDtypeStruct((hidden, D), jnp.bfloat16)
    outs = pl.pallas_call(
        unpack_kernel, out_shape=(rows,) * 3, in_specs=[whole] * len(PARTS), out_specs=(whole,) * 3,
        compiler_params=params(), name="unpack",
    )(*returned)
    return tuple(o[None] for o in outs)


def solution(mesh):
    return jax.shard_map(
        body,
        mesh=mesh,
        in_specs=(
            P("expert", "dp"),
            P("expert", "dp"),
            P("expert", None),
            P("expert", None),
            P("expert", "dp", None),
            P("expert", "dp", None),
            P("expert", "dp", None),
            P(),
        ),
        out_specs=(P("expert", "dp", None), P("expert", "dp", None), P("expert", "dp", None)),
        check_vma=False,
    )
```

```python
import jax
import jax.numpy as jnp
from jax import lax
from jax.experimental import pallas as pl
from jax.experimental.pallas import tpu as pltpu
from jax.sharding import PartitionSpec as P


D = 2048
FF = 1536
MEMBERS = 4
EXPERTS = 64
CLUSTERS = 16
ROWS = 3
PARTS = ((0, 1, 2),)
LANES = 128
TILES = D // LANES
BLOCK = 32
WIDTH = 256
Y, Z = 4, 16
fisher_floor = 1e-06
VMEM_LIMIT = 60 * 1024 * 1024


def swap_matrix():
    row = lax.broadcasted_iota(jnp.int32, (256, 256), 0)
    col = lax.broadcasted_iota(jnp.int32, (256, 256), 1)
    hit = (row // 16 == col % 16) & (row % 16 == col // 16)
    return jnp.where(hit, 1.0, 0.0).astype(jnp.bfloat16)


def dot(left, right):
    return jnp.dot(left, right, preferred_element_type=jnp.float32)


def dot_t(left, right):
    return lax.dot_general(
        left, right, (((1,), (1,)), ((), ())), preferred_element_type=jnp.float32
    )


def picks(rows, cols, of_row):
    row = lax.broadcasted_iota(jnp.int32, (rows, cols), 0)
    col = lax.broadcasted_iota(jnp.int32, (rows, cols), 1)
    return jnp.where(of_row(row) == col, 1.0, 0.0).astype(jnp.bfloat16)


def member_table(belongs):
    shape = (belongs.shape[1] // EXPERTS * CLUSTERS, belongs.shape[1])
    filled = dot(picks(shape[0], CLUSTERS, lambda r: r % CLUSTERS), belongs)
    row = lax.broadcasted_iota(jnp.int32, shape, 0)
    col = lax.broadcasted_iota(jnp.int32, shape, 1)
    return jnp.where(row // CLUSTERS == col // EXPERTS, filled, 0.0).astype(jnp.bfloat16)


def spread_table(belongs):
    shape = (EXPERTS * TILES, TILES * CLUSTERS)
    filled = dot(picks(shape[0], EXPERTS, lambda r: r // TILES), belongs)
    row = lax.broadcasted_iota(jnp.int32, shape, 0)
    col = lax.broadcasted_iota(jnp.int32, shape, 1)
    return jnp.where(row % TILES == col // CLUSTERS, filled, 0.0).astype(jnp.bfloat16)


def turn(left, blocks):
    turned = []
    for i in range(0, len(blocks), 2):
        pair = blocks[i : i + 2]
        both = dot(left, jnp.concatenate(pair, axis=1)).astype(jnp.bfloat16)
        turned += [both[:, n * LANES : (n + 1) * LANES] for n in range(len(pair))]
    return turned


def parts_of():
    for part, groups in enumerate(PARTS):
        for m in range(3):
            for i, j in enumerate(groups):
                yield part, m * len(groups) + i, m, j


def pack_kernel(*refs):
    swap = swap_matrix()
    groups = list(parts_of())
    for kb in range(4):
        stacked = []
        for _, _, m, j in groups:
            rows = slice(64 * j + 16 * kb, 64 * j + 16 * kb + 16)
            tiles = [refs[m][rows, l * LANES : (l + 1) * LANES] for l in range(TILES)]
            stacked.append(jnp.concatenate(tiles, axis=0))
        for (part, q, _, _), block in zip(groups, turn(swap, stacked)):
            refs[3 + part][16 * kb : 16 * kb + 16, 16 * q : 16 * q + 16, :] = block.reshape(
                16, 16, LANES
            )


def unpack_kernel(*refs):
    swap = swap_matrix()
    groups = list(parts_of())
    for kb in range(4):
        stacked = [
            refs[part][16 * kb : 16 * kb + 16, 16 * q : 16 * q + 16, :].reshape(256, LANES)
            for part, q, _, _ in groups
        ]
        for (_, _, m, j), block in zip(groups, turn(swap, stacked)):
            rows = slice(64 * j + 16 * kb, 64 * j + 16 * kb + 16)
            for l in range(TILES):
                refs[len(PARTS) + m][rows, l * LANES : (l + 1) * LANES] = block[
                    16 * l : 16 * l + 16
                ]


def merge_kernel(*refs):
    (packed, route_map, belongs_row, belongs_col) = refs[:4]
    pieces = refs[4:24]
    out, tok, cot, weights, fisher_rows, merged, sems = refs[24:]
    kinds = packed.shape[1] // TILES
    place = lax.axis_index("dp")
    x, core = place // 2, place % 2
    shifts = (0, 3, 1, 2)

    def bring(piece, target, first, shift, c, which, t):
        lane = pl.multiple_of((((x + shift) % 4) * 2 + c) * WIDTH, WIDTH)
        pltpu.make_async_copy(
            piece, target.at[first : first + piece.shape[0], :, pl.ds(lane, WIDTH)],
            sems.at[which, t],
        ).start()

    for t in range(8):
        for side in range(2):
            c = core if side == 0 else 1 - core
            tok_pieces = pieces[10 * side : 10 * side + 5]
            cot_pieces = pieces[10 * side + 5 : 10 * side + 10]
            for i in range(3):
                bring(tok_pieces[i].at[8 * t : 8 * t + 8], tok, 8 * t, shifts[i], c, 0, t)
            far = 8 * (t % 4)
            bring(tok_pieces[3 + t // 4].at[far : far + 8], tok, 8 * t, shifts[3], c, 0, t)
            for h in range(4):
                if t < 6:
                    piece, at = cot_pieces[t // 2], h
                else:
                    piece, at = cot_pieces[3 + h // 2], h % 2
                first = 16 * at + 8 * (t % 2)
                bring(piece.at[first : first + 8], cot, 8 * t, shifts[h], c, 1, t)

    def ready(t):
        for which, target in enumerate((tok, cot)):
            rows = target.at[8 * t : 8 * t + 8]
            pltpu.make_async_copy(rows, rows, sems.at[which, t]).wait()

    swap = swap_matrix()
    for eb in range(4):
        stacked = [
            packed[16 * eb : 16 * eb + 16, 16 * q : 16 * q + 16, :].reshape(256, LANES)
            for q in range(kinds)
        ]
        for q, block in enumerate(turn(swap, stacked)):
            rows = slice(64 * q + 16 * eb, 64 * q + 16 * eb + 16)
            for l in range(TILES):
                weights[rows, l * LANES : (l + 1) * LANES] = block[16 * l : 16 * l + 16]
    third = kinds // 3 * EXPERTS
    table = member_table(belongs_row[...])

    def project(t):
        ready(t)
        at = 8 * t
        tok_rows = tok[pl.ds(at, 8)].reshape(256, D)
        cot_rows = cot[pl.ds(at, 8)].reshape(256, D)
        lane = 256 * t
        share = route_map[:, pl.ds(lane, 256)]
        share = jnp.concatenate([share] * (kinds // 3), axis=0)
        pre = dot_t(weights[0 : 2 * third, :], tok_rows) * (D**-0.5)
        act_grad = dot_t(weights[2 * third :, :], cot_rows) * (FF**-0.5) * share
        gate_pre, up_pre = pre[:third], pre[third:]
        sigmoid = jax.nn.sigmoid(gate_pre)
        silu = gate_pre * sigmoid
        slope = sigmoid * (1.0 + gate_pre * (1.0 - sigmoid))
        gate_grad = act_grad * up_pre * slope
        up_grad = act_grad * silu
        act = silu * up_pre * share
        for m, value in enumerate((gate_grad, up_grad, act)):
            fisher_rows[m * third : (m + 1) * third, pl.ds(lane, 256)] = (value * value).astype(
                jnp.bfloat16
            )

    for t in range(8):
        project(t)

    def merge(f):
        lane = f * WIDTH
        tok_cols = tok[:, :, pl.ds(lane, WIDTH)].reshape(2048, WIDTH)
        cot_cols = cot[:, :, pl.ds(lane, WIDTH)].reshape(2048, WIDTH)
        fisher_in = dot(fisher_rows[0 : 2 * third, :], tok_cols * tok_cols)
        fisher_down = dot(fisher_rows[2 * third :, :], cot_cols * cot_cols)
        fisher = jnp.concatenate(
            [fisher_in.astype(jnp.bfloat16), fisher_down.astype(jnp.bfloat16)], axis=0
        )
        product = fisher.astype(jnp.float32) * weights[:, pl.ds(lane, WIDTH)].astype(jnp.float32)
        sums = dot(table, jnp.concatenate([product.astype(jnp.bfloat16), fisher], axis=1))
        numerator, denominator = sums[:, :WIDTH], sums[:, WIDTH:]
        merged[:, pl.ds(lane, WIDTH)] = (numerator / (denominator + fisher_floor)).astype(
            jnp.bfloat16
        )

    for f in range(8):
        merge(f)
    spread = spread_table(belongs_col[...])
    stacked = [
        jnp.concatenate(
            [merged[16 * q : 16 * q + 16, l * LANES : (l + 1) * LANES] for l in range(TILES)], axis=0
        )
        for q in range(kinds)
    ]
    for eb in range(4):
        for q, block in enumerate(turn(spread[256 * eb : 256 * eb + 256], stacked)):
            out[16 * eb : 16 * eb + 16, 16 * q : 16 * q + 16, :] = block.reshape(16, 16, LANES)


def params():
    return pltpu.CompilerParams(vmem_limit_bytes=VMEM_LIMIT)


def packed_shape(kinds):
    return jax.ShapeDtypeStruct((EXPERTS, kinds * TILES, LANES), jnp.bfloat16)


def expert_pairs(move):
    return [(y * Z + z, move(y, z)[0] * Z + move(y, z)[1]) for y in range(Y) for z in range(Z)]


def dp_pairs(move):
    return [(2 * x + c, move(x, c)[0] * 2 + move(x, c)[1]) for x in range(4) for c in range(2)]


def body(
    tokens, cotangent, routes, route_weights, gate_weight, up_weight, down_weight, cluster_order
):
    hidden = gate_weight.shape[1]
    whole = pl.BlockSpec(memory_space=pltpu.VMEM)
    shapes = tuple(packed_shape(3 * len(groups)) for groups in PARTS)
    packed = pl.pallas_call(
        pack_kernel, out_shape=shapes, in_specs=[whole] * 3, out_specs=(whole,) * len(PARTS),
        compiler_params=params(), name="pack",
    )(gate_weight[0], up_weight[0], down_weight[0])
    cluster = cluster_order // MEMBERS
    clusters = jnp.arange(CLUSTERS, dtype=jnp.int32)
    belongs_col = (cluster[:, None] == jnp.tile(clusters, TILES)[None, :]).astype(jnp.bfloat16)
    belongs_row = (clusters[:, None] == jnp.tile(cluster, 3 * ROWS)[None, :]).astype(jnp.bfloat16)

    chosen = routes[:, :, None] == jnp.arange(EXPERTS, dtype=jnp.int32)[None, None, :]
    share = jnp.sum(jnp.where(chosen, route_weights.astype(jnp.float32)[:, :, None], 0.0), axis=1)
    share = share.astype(jnp.bfloat16)
    share = jnp.concatenate([share[8 * i : 8 * i + 8] for i in range(4)], axis=1)
    block = jnp.concatenate([tokens, share, cotangent], axis=0)[None]

    def along_z(value, shift):
        return lax.ppermute(value, "expert", expert_pairs(lambda y, z: (y, (z + shift) % Z)))

    block = jnp.concatenate([block] + [along_z(block, shift) for shift in (4, 8, 12)], axis=0)
    packed, block, belongs_row, belongs_col = lax.optimization_barrier(
        (packed, block, belongs_row, belongs_col)
    )

    def along_y(value, shift):
        return lax.ppermute(value, "expert", expert_pairs(lambda y, z: ((y + shift) % Y, z)))

    def along_x(value, shift):
        return lax.ppermute(value, "dp", dp_pairs(lambda x, c: ((x + shift) % 4, c)))

    def whole_ring(value, along):
        return jnp.concatenate([value] + [along(value, shift) for shift in (1, -1, 2)], axis=0)

    def split_ring(value, along, beside=None):
        half = value.shape[0] // 2
        before, after = along(value, 1), along(value, -1)
        if beside is not None:
            before, after, beside = lax.optimization_barrier((before, after, beside))
        return (value, before, after, along(before[:half], 1), along(after[half:], -1)), beside

    near_z = [along_z(block, shift) for shift in (1, -1, 2)]
    block = jnp.concatenate([block] + near_z, axis=0)
    received = []
    for part in packed:
        received.append(lax.all_to_all(part, "expert", split_axis=0, concat_axis=0, tiled=True))
    tok_block = whole_ring(block[:, : BLOCK + 8], along_y)
    cot_block = whole_ring(block[:, BLOCK + 8 :], along_x)
    share = tok_block[:, BLOCK:].reshape(EXPERTS, 8, 4, EXPERTS).transpose(3, 0, 2, 1)
    share = share.reshape(EXPERTS, EXPERTS * BLOCK).astype(jnp.float32)
    cot_near, _ = split_ring(cot_block, along_y)
    tok_near, share = split_ring(tok_block[:, :BLOCK], along_x, share)
    near = tok_near + cot_near
    across = dp_pairs(lambda x, c: (x, 1 - c))
    pieces = near + tuple(lax.ppermute(piece, "dp", across) for piece in near)

    anywhere = pl.BlockSpec(memory_space=pl.ANY)
    returned = []
    for n, part in enumerate(received):
        kinds = 3 * len(PARTS[n])
        answer = pl.pallas_call(
            merge_kernel, out_shape=shapes[n],
            in_specs=[whole] * 4 + [anywhere] * 20, out_specs=whole,
            scratch_shapes=[
                pltpu.VMEM((EXPERTS, BLOCK, D), jnp.bfloat16),
                pltpu.VMEM((EXPERTS, BLOCK, D), jnp.bfloat16),
                pltpu.VMEM((kinds * EXPERTS, D), jnp.bfloat16),
                pltpu.VMEM((kinds * EXPERTS, EXPERTS * BLOCK), jnp.bfloat16),
                pltpu.VMEM((kinds * CLUSTERS, D), jnp.bfloat16),
                pltpu.SemaphoreType.DMA((2, 8)),
            ],
            compiler_params=params(),
        )(part, share, belongs_row[:, : kinds * EXPERTS], belongs_col, *pieces)
        returned.append(lax.all_to_all(answer, "expert", split_axis=0, concat_axis=0, tiled=True))
    rows = jax.ShapeDtypeStruct((hidden, D), jnp.bfloat16)
    outs = pl.pallas_call(
        unpack_kernel, out_shape=(rows,) * 3, in_specs=[whole] * len(PARTS), out_specs=(whole,) * 3,
        compiler_params=params(), name="unpack",
    )(*returned)
    return tuple(o[None] for o in outs)


def solution(mesh):
    return jax.shard_map(
        body,
        mesh=mesh,
        in_specs=(
            P("expert", "dp"),
            P("expert", "dp"),
            P("expert", None),
            P("expert", None),
            P("expert", "dp", None),
            P("expert", "dp", None),
            P("expert", "dp", None),
            P(),
        ),
        out_specs=(P("expert", "dp", None), P("expert", "dp", None), P("expert", "dp", None)),
        check_vma=False,
    )
```

```python
import jax
import jax.numpy as jnp
from jax import lax
from jax.experimental import pallas as pl
from jax.experimental.pallas import tpu as pltpu
from jax.sharding import PartitionSpec as P


D = 2048
FF = 1536
MEMBERS = 4
EXPERTS = 64
CLUSTERS = 16
ROWS = 3
PARTS = ((0, 1, 2),)
LANES = 128
TILES = D // LANES
BLOCK = 32
WIDTH = 256
Y, Z = 4, 16
fisher_floor = 1e-06
VMEM_LIMIT = 60 * 1024 * 1024


def swap_matrix():
    row = lax.broadcasted_iota(jnp.int32, (256, 256), 0)
    col = lax.broadcasted_iota(jnp.int32, (256, 256), 1)
    hit = (row // 16 == col % 16) & (row % 16 == col // 16)
    return jnp.where(hit, 1.0, 0.0).astype(jnp.bfloat16)


def dot(left, right):
    return jnp.dot(left, right, preferred_element_type=jnp.float32)


def dot_t(left, right):
    return lax.dot_general(
        left, right, (((1,), (1,)), ((), ())), preferred_element_type=jnp.float32
    )


def picks(rows, cols, of_row):
    row = lax.broadcasted_iota(jnp.int32, (rows, cols), 0)
    col = lax.broadcasted_iota(jnp.int32, (rows, cols), 1)
    return jnp.where(of_row(row) == col, 1.0, 0.0).astype(jnp.bfloat16)


def member_table(belongs):
    shape = (belongs.shape[1] // EXPERTS * CLUSTERS, belongs.shape[1])
    filled = dot(picks(shape[0], CLUSTERS, lambda r: r % CLUSTERS), belongs)
    row = lax.broadcasted_iota(jnp.int32, shape, 0)
    col = lax.broadcasted_iota(jnp.int32, shape, 1)
    return jnp.where(row // CLUSTERS == col // EXPERTS, filled, 0.0).astype(jnp.bfloat16)


def spread_table(belongs):
    shape = (EXPERTS * TILES, TILES * CLUSTERS)
    filled = dot(picks(shape[0], EXPERTS, lambda r: r // TILES), belongs)
    row = lax.broadcasted_iota(jnp.int32, shape, 0)
    col = lax.broadcasted_iota(jnp.int32, shape, 1)
    return jnp.where(row % TILES == col // CLUSTERS, filled, 0.0).astype(jnp.bfloat16)


def turn(left, blocks):
    turned = []
    for i in range(0, len(blocks), 2):
        pair = blocks[i : i + 2]
        both = dot(left, jnp.concatenate(pair, axis=1)).astype(jnp.bfloat16)
        turned += [both[:, n * LANES : (n + 1) * LANES] for n in range(len(pair))]
    return turned


def parts_of():
    for part, groups in enumerate(PARTS):
        for m in range(3):
            for i, j in enumerate(groups):
                yield part, m * len(groups) + i, m, j


def pack_kernel(*refs):
    swap = swap_matrix()
    groups = list(parts_of())
    for kb in range(4):
        stacked = []
        for _, _, m, j in groups:
            rows = slice(64 * j + 16 * kb, 64 * j + 16 * kb + 16)
            tiles = [refs[m][rows, l * LANES : (l + 1) * LANES] for l in range(TILES)]
            stacked.append(jnp.concatenate(tiles, axis=0))
        for (part, q, _, _), block in zip(groups, turn(swap, stacked)):
            refs[3 + part][16 * kb : 16 * kb + 16, 16 * q : 16 * q + 16, :] = block.reshape(
                16, 16, LANES
            )


def unpack_kernel(*refs):
    swap = swap_matrix()
    groups = list(parts_of())
    for kb in range(4):
        stacked = [
            refs[part][16 * kb : 16 * kb + 16, 16 * q : 16 * q + 16, :].reshape(256, LANES)
            for part, q, _, _ in groups
        ]
        for (_, _, m, j), block in zip(groups, turn(swap, stacked)):
            rows = slice(64 * j + 16 * kb, 64 * j + 16 * kb + 16)
            for l in range(TILES):
                refs[len(PARTS) + m][rows, l * LANES : (l + 1) * LANES] = block[
                    16 * l : 16 * l + 16
                ]


def merge_kernel(*refs):
    (packed, route_map, belongs_row, belongs_col) = refs[:4]
    pieces = refs[4:24]
    out, tok, cot, weights, fisher_rows, merged, sems = refs[24:]
    kinds = packed.shape[1] // TILES
    place = lax.axis_index("dp")
    x, core = place // 2, place % 2
    shifts = (0, 3, 1, 2)

    def bring(piece, target, first, shift, c, which, t):
        lane = pl.multiple_of((((x + shift) % 4) * 2 + c) * WIDTH, WIDTH)
        pltpu.make_async_copy(
            piece, target.at[first : first + piece.shape[0], :, pl.ds(lane, WIDTH)],
            sems.at[which, t],
        ).start()

    for t in range(8):
        for side in range(2):
            c = core if side == 0 else 1 - core
            tok_pieces = pieces[10 * side : 10 * side + 5]
            cot_pieces = pieces[10 * side + 5 : 10 * side + 10]
            for i in range(3):
                bring(tok_pieces[i].at[8 * t : 8 * t + 8], tok, 8 * t, shifts[i], c, 0, t)
            far = 8 * (t % 4)
            bring(tok_pieces[3 + t // 4].at[far : far + 8], tok, 8 * t, shifts[3], c, 0, t)
            for h in range(4):
                if t < 6:
                    piece, at = cot_pieces[t // 2], h
                else:
                    piece, at = cot_pieces[3 + h // 2], h % 2
                first = 16 * at + 8 * (t % 2)
                bring(piece.at[first : first + 8], cot, 8 * t, shifts[h], c, 1, t)

    def ready(t):
        for which, target in enumerate((tok, cot)):
            rows = target.at[8 * t : 8 * t + 8]
            pltpu.make_async_copy(rows, rows, sems.at[which, t]).wait()

    swap = swap_matrix()
    for eb in range(4):
        stacked = [
            packed[16 * eb : 16 * eb + 16, 16 * q : 16 * q + 16, :].reshape(256, LANES)
            for q in range(kinds)
        ]
        for q, block in enumerate(turn(swap, stacked)):
            rows = slice(64 * q + 16 * eb, 64 * q + 16 * eb + 16)
            for l in range(TILES):
                weights[rows, l * LANES : (l + 1) * LANES] = block[16 * l : 16 * l + 16]
    third = kinds // 3 * EXPERTS
    table = member_table(belongs_row[...])

    def project(t):
        ready(t)
        at = 8 * t
        tok_rows = tok[pl.ds(at, 8)].reshape(256, D)
        cot_rows = cot[pl.ds(at, 8)].reshape(256, D)
        lane = 256 * t
        share = route_map[:, pl.ds(lane, 256)]
        share = jnp.concatenate([share] * (kinds // 3), axis=0)
        pre = dot_t(weights[0 : 2 * third, :], tok_rows) * (D**-0.5)
        act_grad = dot_t(weights[2 * third :, :], cot_rows) * (FF**-0.5) * share
        gate_pre, up_pre = pre[:third], pre[third:]
        sigmoid = jax.nn.sigmoid(gate_pre)
        silu = gate_pre * sigmoid
        slope = sigmoid * (1.0 + gate_pre * (1.0 - sigmoid))
        gate_grad = act_grad * up_pre * slope
        up_grad = act_grad * silu
        act = silu * up_pre * share
        for m, value in enumerate((gate_grad, up_grad, act)):
            fisher_rows[m * third : (m + 1) * third, pl.ds(lane, 256)] = (value * value).astype(
                jnp.bfloat16
            )

    for t in range(8):
        project(t)

    def merge(f):
        lane = f * WIDTH
        tok_cols = tok[:, :, pl.ds(lane, WIDTH)].reshape(2048, WIDTH)
        cot_cols = cot[:, :, pl.ds(lane, WIDTH)].reshape(2048, WIDTH)
        fisher_in = dot(fisher_rows[0 : 2 * third, :], tok_cols * tok_cols)
        fisher_down = dot(fisher_rows[2 * third :, :], cot_cols * cot_cols)
        fisher = jnp.concatenate(
            [fisher_in.astype(jnp.bfloat16), fisher_down.astype(jnp.bfloat16)], axis=0
        )
        product = fisher.astype(jnp.float32) * weights[:, pl.ds(lane, WIDTH)].astype(jnp.float32)
        sums = dot(table, jnp.concatenate([product.astype(jnp.bfloat16), fisher], axis=1))
        numerator, denominator = sums[:, :WIDTH], sums[:, WIDTH:]
        merged[:, pl.ds(lane, WIDTH)] = (numerator / (denominator + fisher_floor)).astype(
            jnp.bfloat16
        )

    for f in range(8):
        merge(f)
    spread = spread_table(belongs_col[...])
    stacked = [
        jnp.concatenate(
            [merged[16 * q : 16 * q + 16, l * LANES : (l + 1) * LANES] for l in range(TILES)], axis=0
        )
        for q in range(kinds)
    ]
    for eb in range(4):
        for q, block in enumerate(turn(spread[256 * eb : 256 * eb + 256], stacked)):
            out[16 * eb : 16 * eb + 16, 16 * q : 16 * q + 16, :] = block.reshape(16, 16, LANES)


def params():
    return pltpu.CompilerParams(vmem_limit_bytes=VMEM_LIMIT)


def packed_shape(kinds):
    return jax.ShapeDtypeStruct((EXPERTS, kinds * TILES, LANES), jnp.bfloat16)


def expert_pairs(move):
    return [(y * Z + z, move(y, z)[0] * Z + move(y, z)[1]) for y in range(Y) for z in range(Z)]


def dp_pairs(move):
    return [(2 * x + c, move(x, c)[0] * 2 + move(x, c)[1]) for x in range(4) for c in range(2)]


def body(
    tokens, cotangent, routes, route_weights, gate_weight, up_weight, down_weight, cluster_order
):
    hidden = gate_weight.shape[1]
    whole = pl.BlockSpec(memory_space=pltpu.VMEM)
    shapes = tuple(packed_shape(3 * len(groups)) for groups in PARTS)
    packed = pl.pallas_call(
        pack_kernel, out_shape=shapes, in_specs=[whole] * 3, out_specs=(whole,) * len(PARTS),
        compiler_params=params(), name="pack",
    )(gate_weight[0], up_weight[0], down_weight[0])
    cluster = cluster_order // MEMBERS
    clusters = jnp.arange(CLUSTERS, dtype=jnp.int32)
    belongs_col = (cluster[:, None] == jnp.tile(clusters, TILES)[None, :]).astype(jnp.bfloat16)
    belongs_row = (clusters[:, None] == jnp.tile(cluster, 3 * ROWS)[None, :]).astype(jnp.bfloat16)

    ids = jnp.arange(EXPERTS, dtype=jnp.int32)[None, :, None]
    weight = route_weights.T.astype(jnp.float32)[:, None, :]
    share = jnp.sum(jnp.where(routes.T[:, None, :] == ids, weight, 0.0), axis=0)
    share = share.astype(jnp.bfloat16)
    share = jnp.concatenate([share[8 * i : 8 * i + 8] for i in range(8)], axis=1)
    block = jnp.concatenate([tokens, share, cotangent], axis=0)[None]

    def along_z(value, shift):
        return lax.ppermute(value, "expert", expert_pairs(lambda y, z: (y, (z + shift) % Z)))

    block = jnp.concatenate([block] + [along_z(block, shift) for shift in (4, 8, 12)], axis=0)
    packed, block = lax.optimization_barrier((packed, block))

    def along_y(value, shift):
        return lax.ppermute(value, "expert", expert_pairs(lambda y, z: ((y + shift) % Y, z)))

    def along_x(value, shift):
        return lax.ppermute(value, "dp", dp_pairs(lambda x, c: ((x + shift) % 4, c)))

    def whole_ring(value, along):
        return jnp.concatenate([value] + [along(value, shift) for shift in (1, -1, 2)], axis=0)

    def split_ring(value, along, beside=None):
        half = value.shape[0] // 2
        before, after = along(value, 1), along(value, -1)
        if beside is not None:
            before, after, beside = lax.optimization_barrier((before, after, beside))
        return (value, before, after, along(before[:half], 1), along(after[half:], -1)), beside

    near_z = [along_z(block, shift) for shift in (1, -1, 2)]
    block = jnp.concatenate([block] + near_z, axis=0)
    received = []
    for part in packed:
        received.append(lax.all_to_all(part, "expert", split_axis=0, concat_axis=0, tiled=True))
    tok_block = whole_ring(block[:, : BLOCK + 8], along_y)
    cot_block = whole_ring(block[:, BLOCK + 8 :], along_x)
    share = tok_block[:, BLOCK:].reshape(EXPERTS, 8, 8, BLOCK).transpose(2, 1, 0, 3)
    share = share.reshape(EXPERTS, EXPERTS * BLOCK).astype(jnp.float32)
    cot_near, _ = split_ring(cot_block, along_y)
    tables = (share, belongs_row, belongs_col)
    tok_near, tables = split_ring(tok_block[:, :BLOCK], along_x, tables)
    share, belongs_row, belongs_col = tables
    near = tok_near + cot_near
    across = dp_pairs(lambda x, c: (x, 1 - c))
    pieces = near + tuple(lax.ppermute(piece, "dp", across) for piece in near)

    anywhere = pl.BlockSpec(memory_space=pl.ANY)
    returned = []
    for n, part in enumerate(received):
        kinds = 3 * len(PARTS[n])
        answer = pl.pallas_call(
            merge_kernel, out_shape=shapes[n],
            in_specs=[whole] * 4 + [anywhere] * 20, out_specs=whole,
            scratch_shapes=[
                pltpu.VMEM((EXPERTS, BLOCK, D), jnp.bfloat16),
                pltpu.VMEM((EXPERTS, BLOCK, D), jnp.bfloat16),
                pltpu.VMEM((kinds * EXPERTS, D), jnp.bfloat16),
                pltpu.VMEM((kinds * EXPERTS, EXPERTS * BLOCK), jnp.bfloat16),
                pltpu.VMEM((kinds * CLUSTERS, D), jnp.bfloat16),
                pltpu.SemaphoreType.DMA((2, 8)),
            ],
            compiler_params=params(),
        )(part, share, belongs_row[:, : kinds * EXPERTS], belongs_col, *pieces)
        returned.append(lax.all_to_all(answer, "expert", split_axis=0, concat_axis=0, tiled=True))
    rows = jax.ShapeDtypeStruct((hidden, D), jnp.bfloat16)
    outs = pl.pallas_call(
        unpack_kernel, out_shape=(rows,) * 3, in_specs=[whole] * len(PARTS), out_specs=(whole,) * 3,
        compiler_params=params(), name="unpack",
    )(*returned)
    return tuple(o[None] for o in outs)


def solution(mesh):
    return jax.shard_map(
        body,
        mesh=mesh,
        in_specs=(
            P("expert", "dp"),
            P("expert", "dp"),
            P("expert", None),
            P("expert", None),
            P("expert", "dp", None),
            P("expert", "dp", None),
            P("expert", "dp", None),
            P(),
        ),
        out_specs=(P("expert", "dp", None), P("expert", "dp", None), P("expert", "dp", None)),
        check_vma=False,
    )
```
